256 devices in a mesh: wide: 64 (over z, y, core), narrow: 4 (over x).
Axes of the slice: x: 4, y: 4, z: 8, core: 2. Of those that a mesh axis runs over, the one named last changes fastest.
Arguments:
- stored_amps: float32 [1024, 16384], P('wide', 'narrow'), may hold values from -6 to 6
- integrals: float32 [16384, 16384], P('narrow', 'wide'), may hold values from -0.046875 to 0.046875
- pair_counts: int32 [4], replicated, may hold values from 2048 to 4096, as said below
- block_map: int32 [64], replicated, may hold values from 0 to 63, each once
Outputs:
- cycle_out: float32 [1024, 16384], P('wide', 'narrow')
The draws below stay inside these ranges and needn't reach their ends.
Inputs may be any that keep to these rules, and one draw needn't show every extreme that they name: `pair_counts`: each count lies between half of 4096 and 4096; one count equals 4096. `block_map`: a permutation of the indices of wide.
All inputs are finite; a program needn't handle non-finite values.
Results may differ from the reference program's by a relative error of at most 0.000086.
Values sent between devices are 32-bit elements; how exact they have to be, the bound alone decides.
No kernel may reach another device: no remote copies, remote signals or barrier semaphores. Data moves between devices by JAX's collectives and lax.ppermute only.
A program may use at most 64 MiB of HBM per device.

```python
import jax
import jax.numpy as jnp
from jax import lax

PB = 4096
Q = 16384
BR = 8
NL = 2
R = 1024
P_SIZE = 16384
G = 64
N_WIDE = 64
N_NARROW = 4


def draw_pair_counts(key, part):
    first, second = jax.random.split(jax.random.fold_in(key, 11))
    values = jax.random.randint(first, (4,), PB // 2, PB + 1)
    chosen = jax.random.randint(second, (), 0, 4)
    return jnp.where(jnp.arange(4) == chosen, PB, values).astype(jnp.int32)


def steps_of(stream_key, dims, cuts, smallest, largest):
    loudness = 1.0
    for position, parts in cuts:
        heights = jax.random.uniform(jax.random.fold_in(jax.random.fold_in(stream_key, 6), position), (parts,), jnp.float32, smallest / len(cuts), largest / len(cuts))
        loudness = loudness * jnp.repeat(jnp.exp(heights), dims[position] // parts).reshape((-1,) + (1,) * (len(dims) - 1 - position))
    return loudness


def scatter_about(rng, shape, scale, reach, pieces=(), held_as=jnp.bfloat16):
    drawn = scale * jax.random.normal(rng, shape, jnp.float32)
    if pieces:
        drawn = drawn * steps_of(rng, shape, pieces, -0.22, 0.18)
    return jnp.clip(drawn, -reach, reach).astype(held_as)


def setup_inputs(seed: int = 0) -> dict:
    keys = jax.random.split(jax.random.key(seed), 5)
    stored_amps = scatter_about(keys[0], (R, P_SIZE), 1.0, 6.0, ((0, 64), (1, 4)), jnp.float32)
    integrals = scatter_about(keys[1], (P_SIZE, Q), P_SIZE ** -0.5, 0.046875, ((0, 4), (1, 64)), jnp.float32)
    pair_counts = draw_pair_counts(jax.random.fold_in(keys[4], 71), 0)
    block_map = jax.random.permutation(keys[3], N_WIDE).astype(jnp.int32)
    return {"stored_amps": stored_amps, "integrals": integrals, "pair_counts": pair_counts, "block_map": block_map}


def reference(stored_amps, integrals, pair_counts, block_map):
    blocks = stored_amps.reshape(N_WIDE, NL, BR, P_SIZE)
    blocks = jnp.take(blocks, block_map, axis=0)
    tamp = jnp.transpose(blocks, (1, 0, 2, 3)).reshape(R, P_SIZE)
    columns = jnp.arange(P_SIZE, dtype=jnp.int32)
    limit = jnp.take(pair_counts, columns // PB)
    tamp = jnp.where((columns % PB < limit)[None, :], tamp, jnp.float32(0.0))
    cycle = jnp.dot(tamp, integrals, precision=lax.Precision.HIGHEST, preferred_element_type=jnp.float32)
    grouped = cycle.reshape(R, N_WIDE, N_NARROW, G)
    return jnp.transpose(grouped, (0, 2, 1, 3)).reshape(R, Q)
```

```python
import jax
import jax.numpy as jnp
from jax import lax
from jax.sharding import PartitionSpec as P

NZ, NY, NC, NX = 8, 4, 2, 4
BR = 8
G = 64


def wide_pairs(dz, dy, dc=0):
    pairs = []
    for z in range(NZ):
        for y in range(NY):
            for c in range(NC):
                source = (z * NY + y) * NC + c
                target = (((z + dz) % NZ) * NY + (y + dy) % NY) * NC + (c + dc) % NC
                pairs.append((source, target))
    return pairs


def along_z(block, step):
    return lax.ppermute(block, "wide", wide_pairs(step, 0))


def along_y(block, step):
    return lax.ppermute(block, "wide", wide_pairs(0, step))


def other_core(block):
    return lax.ppermute(block, "wide", wide_pairs(0, 0, 1))


def along_x(block, step):
    return lax.ppermute(block, "narrow", [(i, (i + step) % NX) for i in range(NX)])


def on_device(stored_amps, integrals, pair_counts, block_map):
    place = lax.axis_index("wide")
    layer = lax.axis_index("narrow")
    core = place % NC
    my_y = (place // NC) % NY
    my_z = place // (NC * NY)
    width = stored_amps.shape[1]
    half = width // 2

    live = jnp.arange(width, dtype=jnp.int32)[:, None] < pair_counts[layer]
    integrals = jnp.where(live, integrals, jnp.float32(0.0))
    theirs = other_core(integrals)

    top, low = stored_amps[:BR], stored_amps[BR:]

    ya, yb = along_y(low, 1), along_y(low, -1)
    za, zb = along_z(top, 1), along_z(top, -1)
    yc = jnp.concatenate([along_y(ya[:, :half], 1), along_y(yb[:, half:], -1)], axis=1)
    row = jnp.concatenate([low, ya, yb, yc], axis=0)
    first = jnp.concatenate([top, za, zb], axis=0)
    zc, zd = along_z(za, 1), along_z(zb, -1)
    fa, fb = along_y(first, 1), along_y(first, -1)
    ra, rb = along_z(row, 1), along_z(row, -1)
    ze, zf = along_z(zc, 1), along_z(zd, -1)
    zg = jnp.concatenate([along_z(ze[:, :half], 1), along_z(zf[:, half:], -1)], axis=1)
    second = jnp.concatenate([zc, zd, ze, zf, zg], axis=0)
    fc = jnp.concatenate([along_y(fa[:, :half], 1), along_y(fb[:, half:], -1)], axis=1)
    sa, sb = along_y(second, 1), along_y(second, -1)
    rc, rd = along_z(ra, 1), along_z(rb, -1)
    re, rf = along_z(rc, 1), along_z(rd, -1)
    sc = jnp.concatenate([along_y(sa[:, :half], 1), along_y(sb[:, half:], -1)], axis=1)
    rg = jnp.concatenate([along_z(re[:, :half], 1), along_z(rf[:, half:], -1)], axis=1)

    rows = jnp.concatenate(
        [first, second, fa, sa, fb, sb, fc, sc, row, ra, rb, rc, rd, re, rf, rg], axis=0
    )

    def times(held):
        return jnp.dot(
            rows, held, precision=lax.Precision.HIGH, preferred_element_type=jnp.float32
        )

    mine, others = times(integrals), times(theirs)
    even = jnp.where(core == 0, mine, others)
    odd = jnp.where(core == 0, others, mine)
    count = rows.shape[0]
    chunks = jnp.concatenate(
        [even.reshape(count, NX, G), odd.reshape(count, NX, G)], axis=2
    )
    chunks = jnp.transpose(chunks, (1, 0, 2))

    def chunk(step):
        return lax.dynamic_index_in_dim(chunks, (layer + step) % NX, 0, keepdims=False)

    total = chunk(0)
    for step in (1, 3, 2):
        total = total + along_x(chunk(step), step)

    sibling = other_core(total)
    both = jnp.stack([jnp.where(core == 0, total, sibling), jnp.where(core == 0, sibling, total)])
    blocks = both.reshape(NC * (count // BR), BR, 2 * G)

    target = jnp.arange(NZ * NY * NC, dtype=jnp.int32)
    pairs = target.shape[0] // 2
    owner = block_map[2 * (target % pairs) + core]
    slot_z = jnp.array([0, 2, 4, 6, 7, 5, 3, 1], jnp.int32)
    slot_y = jnp.array([0, 2, 3, 1], jnp.int32)
    kz = slot_z[(owner // (NC * NY) - my_z) % NZ]
    ky = slot_y[((owner // NC) % NY - my_y) % NY]
    where_top = ky * NZ + kz
    where_low = NZ * NY + kz * NY + ky
    at = jnp.where(target < pairs, where_top, where_low) + (owner % NC) * (2 * NZ * NY)
    sent = jnp.take(blocks, at, axis=0, mode="clip")
    got = lax.all_to_all(sent, "wide", split_axis=0, concat_axis=0, tiled=True)
    got = got.reshape(NZ * NY, NC, BR, 2 * G)
    return jnp.transpose(got, (1, 2, 0, 3)).reshape(NC * BR, NZ * NY * 2 * G)


def solution(mesh):
    placed = (P("wide", "narrow"), P("narrow", "wide"), P(), P())
    return jax.shard_map(
        on_device, mesh=mesh, in_specs=placed, out_specs=P("wide", "narrow"), check_vma=False
    )
```

```python
import jax
import jax.numpy as jnp
from jax import lax
from jax.sharding import PartitionSpec as P

NZ, NY, NC, NX = 8, 4, 2, 4
BR = 8
G = 64


def wide_pairs(dz, dy, swap=False):
    pairs = []
    for z in range(NZ):
        for y in range(NY):
            for c in range(NC):
                way = 1 if c == 0 else -1
                source = (z * NY + y) * NC + c
                chip = ((z + way * dz) % NZ) * NY + (y + way * dy) % NY
                pairs.append((source, chip * NC + (1 - c if swap else c)))
    return pairs


def along_z(block):
    return lax.ppermute(block, "wide", wide_pairs(1, 0))


def along_y(block):
    return lax.ppermute(block, "wide", wide_pairs(0, 1))


def other_core(block):
    return lax.ppermute(block, "wide", wide_pairs(0, 0, True))


def along_x(block, step):
    return lax.ppermute(block, "narrow", [(i, (i + step) % NX) for i in range(NX)])


def after(block, *earlier):
    return lax.optimization_barrier((block, *earlier))[0]


def halves(block):
    high = lax.reduce_precision(block, 8, 7)
    return high.astype(jnp.bfloat16), (block - high).astype(jnp.bfloat16)


def on_device(stored_amps, integrals, pair_counts, block_map):
    place = lax.axis_index("wide")
    layer = lax.axis_index("narrow")
    core = place % NC
    my_y = (place // NC) % NY
    my_z = place // (NC * NY)
    width = stored_amps.shape[1]

    sibling = other_core(stored_amps)
    theirs = other_core(after(integrals, sibling))
    top, low = stored_amps[:BR], stored_amps[BR:]

    def by_core(mine, others):
        return jnp.concatenate(
            [jnp.where(core == 0, mine, others), jnp.where(core == 0, others, mine)], axis=0
        )

    tops = by_core(top, sibling[:BR])
    lows = by_core(low, sibling[BR:])

    def mine_of(block):
        size = block.shape[0] // NC
        return lax.dynamic_slice_in_dim(block, core * size, size, 0)

    live = jnp.arange(width, dtype=jnp.int32)[:, None] < pair_counts[layer]
    held = jnp.where(live, jnp.concatenate([integrals, theirs], axis=1), jnp.float32(0.0))
    held_high, held_low = halves(held)

    def times(pieces):
        high, low_part = halves(jnp.concatenate(pieces, axis=0))
        count = high.shape[0]
        big = jnp.dot(
            jnp.concatenate([high, low_part], axis=0),
            held_high,
            preferred_element_type=jnp.float32,
        )
        small = jnp.dot(high, held_low, preferred_element_type=jnp.float32)
        return big[:count] + (big[count:] + small)

    t1 = along_z(tops)
    l1 = along_y(lows)
    t2 = along_z(t1)
    l2 = along_y(mine_of(l1))
    first = jnp.concatenate([top, t1], axis=0)
    f1 = along_y(after(first, l1))
    row_own = jnp.concatenate([low, l1, l2], axis=0)
    row_other = other_core(row_own)
    t3 = along_z(t2)
    a1 = along_z(after(row_own, t2))
    t4 = along_z(mine_of(t3))
    second = jnp.concatenate([t2, t3, t4], axis=0)
    b1 = along_z(after(row_other, t3))
    f2 = along_y(after(f1, t3))
    s1 = along_y(second)
    a2 = along_z(after(a1, held_high, held_low))
    f3 = along_y(f2)
    b2 = along_z(b1)
    s2 = along_y(s1)
    near = times([first, second, f1, s1, row_own, by_core(a1, b1)])
    a3 = along_z(a2)
    b3 = along_z(after(b2, near))
    s3 = along_y(after(s2, near))
    middle = times([f2, s2, by_core(a2, b2)])
    a4 = along_z(after(a3, middle))
    parts = [near, middle, times([f3, s3, by_core(a3, b3), a4])]
    cycle = jnp.concatenate(parts, axis=0)
    count = cycle.shape[0]
    span = NX * G
    chunks = jnp.stack(
        [
            jnp.concatenate(
                [cycle[:, a * G : (a + 1) * G], cycle[:, span + a * G : span + (a + 1) * G]], axis=1
            )
            for a in range(NX)
        ]
    )

    def chunk(step):
        return lax.dynamic_index_in_dim(chunks, (layer + step) % NX, 0, keepdims=False)

    total = chunk(0)
    for step in (1, 3, 2):
        total = total + along_x(chunk(step), step)
    total = jnp.where(core == 0, total, jnp.roll(total, G, axis=1))

    blocks = by_core(total, other_core(total)).reshape(NC * (count // BR), BR, 2 * G)

    target = jnp.arange(NZ * NY * NC, dtype=jnp.int32)
    pairs = target.shape[0] // 2
    owner = block_map[2 * (target % pairs) + core]
    their_core = owner % NC
    dz = (my_z - owner // (NC * NY)) % NZ
    dy = (my_y - (owner // NC) % NY) % NY
    is_top = target < pairs
    unit_low = jnp.array([0, 1, 3, 5], jnp.int32)[dy] + their_core * jnp.array(
        [4, 1, 4, 1], jnp.int32
    )[dy]
    side = jnp.where(is_top, their_core, unit_low // 4)
    holder = jnp.where(dz % 4 == 0, side, dz // 4)
    steps_z = jnp.where(holder == 0, dz, (NZ - dz) % NZ)
    steps_y = jnp.where(holder == 0, dy, (NY - dy) % NY)
    top_base = jnp.array([0, 8, 28, 44], jnp.int32)[steps_y]
    top_unit = jnp.where(
        steps_z == 0, 0, jnp.where(steps_z == 4, 7, 2 * steps_z - 1 + their_core)
    )
    low_base = jnp.array([16, 20, 36, 52, 60], jnp.int32)[steps_z]
    low_unit = jnp.where(steps_z % 4 == 0, unit_low % 4, unit_low)
    at = jnp.where(is_top, top_base + top_unit, low_base + low_unit) + holder * (count // BR)
    sent = jnp.take(blocks, at, axis=0, mode="clip")
    got = lax.all_to_all(sent, "wide", split_axis=0, concat_axis=0, tiled=True)
    got = got.reshape(NZ * NY, NC, BR, 2 * G)
    return jnp.transpose(got, (1, 2, 0, 3)).reshape(NC * BR, NZ * NY * 2 * G)


def solution(mesh):
    placed = (P("wide", "narrow"), P("narrow", "wide"), P(), P())
    return jax.shard_map(
        on_device, mesh=mesh, in_specs=placed, out_specs=P("wide", "narrow"), check_vma=False
    )
```

```python
import jax
import jax.numpy as jnp
from jax import lax
from jax.sharding import PartitionSpec as P

NZ, NY, NC, NX = 8, 4, 2, 4
BR = 8
G = 64


def wide_pairs(dz, dy, swap=False):
    pairs = []
    for z in range(NZ):
        for y in range(NY):
            for c in range(NC):
                way = 1 if c == 0 else -1
                source = (z * NY + y) * NC + c
                chip = ((z + way * dz) % NZ) * NY + (y + way * dy) % NY
                pairs.append((source, chip * NC + (1 - c if swap else c)))
    return pairs


def along_z(block):
    return lax.ppermute(block, "wide", wide_pairs(1, 0))


def along_y(block):
    return lax.ppermute(block, "wide", wide_pairs(0, 1))


def other_core(block):
    return lax.ppermute(block, "wide", wide_pairs(0, 0, True))


def along_x(block, step):
    return lax.ppermute(block, "narrow", [(i, (i + step) % NX) for i in range(NX)])


def after(block, *earlier):
    return lax.optimization_barrier((block, *earlier))[0]


def halves(block):
    high = lax.reduce_precision(block, 8, 7)
    return high.astype(jnp.bfloat16), (block - high).astype(jnp.bfloat16)


def on_device(stored_amps, integrals, pair_counts, block_map):
    place = lax.axis_index("wide")
    layer = lax.axis_index("narrow")
    core = place % NC
    my_y = (place // NC) % NY
    my_z = place // (NC * NY)
    width = stored_amps.shape[1]

    sibling = other_core(stored_amps)
    theirs = other_core(after(integrals, sibling))
    top, low = stored_amps[:BR], stored_amps[BR:]

    def by_core(mine, others):
        return jnp.concatenate(
            [jnp.where(core == 0, mine, others), jnp.where(core == 0, others, mine)], axis=0
        )

    tops = by_core(top, sibling[:BR])
    lows = by_core(low, sibling[BR:])

    def mine_of(block):
        size = block.shape[0] // NC
        return lax.dynamic_slice_in_dim(block, core * size, size, 0)

    live = jnp.arange(width, dtype=jnp.int32)[:, None] < pair_counts[layer]
    held = jnp.where(live, jnp.concatenate([integrals, theirs], axis=1), jnp.float32(0.0))
    held_high, held_low = halves(held)

    def times(pieces):
        high, low_part = halves(jnp.concatenate(pieces, axis=0))
        count = high.shape[0]
        big = jnp.dot(
            jnp.concatenate([high, low_part], axis=0),
            held_high,
            preferred_element_type=jnp.float32,
        )
        small = jnp.dot(high, held_low, preferred_element_type=jnp.float32)
        return big[:count] + (big[count:] + small)

    t1 = along_z(tops)
    l1 = along_y(lows)
    t2 = along_z(t1)
    l2 = along_y(mine_of(l1))
    first = jnp.concatenate([top, t1], axis=0)
    f1 = along_y(after(first, l1))
    row_own = jnp.concatenate([low, l1, l2], axis=0)
    row_other = other_core(row_own)
    t3 = along_z(t2)
    a1 = along_z(after(row_own, t2))
    t4 = along_z(mine_of(t3))
    second = jnp.concatenate([t2, t3, t4], axis=0)
    b1 = along_z(after(row_other, t3))
    f2 = along_y(after(f1, t3))
    s1 = along_y(second)
    a2 = along_z(a1)
    f3 = along_y(f2)
    b2 = along_z(b1)
    s2 = along_y(s1)
    near = times([first, second, f1, s1, row_own, by_core(a1, b1)])
    a3 = along_z(a2)
    b3 = along_z(b2)
    s3 = along_y(after(s2, near))
    middle = times([f2, s2, by_core(a2, b2)])
    a4 = along_z(after(a3, middle))
    span = NX * G

    def layer_sum(cycle):
        chunks = jnp.stack(
            [
                jnp.concatenate(
                    [cycle[:, a * G : (a + 1) * G], cycle[:, span + a * G : span + (a + 1) * G]],
                    axis=1,
                )
                for a in range(NX)
            ]
        )

        def chunk(step):
            return lax.dynamic_index_in_dim(chunks, (layer + step) % NX, 0, keepdims=False)

        total = chunk(0)
        for step in (1, 3, 2):
            total = total + along_x(chunk(step), step)
        return total

    early = layer_sum(jnp.concatenate([near, middle], axis=0))
    late = layer_sum(times([f3, s3, by_core(a3, b3), a4]))
    total = jnp.concatenate([early, late], axis=0)
    count = total.shape[0]
    total = jnp.where(core == 0, total, jnp.roll(total, G, axis=1))

    blocks = by_core(total, other_core(total)).reshape(NC * (count // BR), BR, 2 * G)

    target = jnp.arange(NZ * NY * NC, dtype=jnp.int32)
    pairs = target.shape[0] // 2
    owner = block_map[2 * (target % pairs) + core]
    their_core = owner % NC
    dz = (my_z - owner // (NC * NY)) % NZ
    dy = (my_y - (owner // NC) % NY) % NY
    is_top = target < pairs
    unit_low = jnp.array([0, 1, 3, 5], jnp.int32)[dy] + their_core * jnp.array(
        [4, 1, 4, 1], jnp.int32
    )[dy]
    side = jnp.where(is_top, their_core, unit_low // 4)
    holder = jnp.where(dz % 4 == 0, side, dz // 4)
    steps_z = jnp.where(holder == 0, dz, (NZ - dz) % NZ)
    steps_y = jnp.where(holder == 0, dy, (NY - dy) % NY)
    top_base = jnp.array([0, 8, 28, 44], jnp.int32)[steps_y]
    top_unit = jnp.where(
        steps_z == 0, 0, jnp.where(steps_z == 4, 7, 2 * steps_z - 1 + their_core)
    )
    low_base = jnp.array([16, 20, 36, 52, 60], jnp.int32)[steps_z]
    low_unit = jnp.where(steps_z % 4 == 0, unit_low % 4, unit_low)
    at = jnp.where(is_top, top_base + top_unit, low_base + low_unit) + holder * (count // BR)
    sent = jnp.take(blocks, at, axis=0, mode="clip")
    got = lax.all_to_all(sent, "wide", split_axis=0, concat_axis=0, tiled=True)
    got = got.reshape(NZ * NY, NC, BR, 2 * G)
    return jnp.transpose(got, (1, 2, 0, 3)).reshape(NC * BR, NZ * NY * 2 * G)


def solution(mesh):
    placed = (P("wide", "narrow"), P("narrow", "wide"), P(), P())
    return jax.shard_map(
        on_device, mesh=mesh, in_specs=placed, out_specs=P("wide", "narrow"), check_vma=False
    )
```

```python
import jax
import jax.numpy as jnp
from jax import lax
from jax.sharding import PartitionSpec as P

NZ, NY, NC, NX = 8, 4, 2, 4
BR = 8
G = 64


def wide_pairs(dz, dy, swap=False):
    pairs = []
    for z in range(NZ):
        for y in range(NY):
            for c in range(NC):
                way = 1 if c == 0 else -1
                source = (z * NY + y) * NC + c
                chip = ((z + way * dz) % NZ) * NY + (y + way * dy) % NY
                pairs.append((source, chip * NC + (1 - c if swap else c)))
    return pairs


def along_z(block):
    return lax.ppermute(block, "wide", wide_pairs(1, 0))


def along_y(block):
    return lax.ppermute(block, "wide", wide_pairs(0, 1))


def other_core(block):
    return lax.ppermute(block, "wide", wide_pairs(0, 0, True))


def along_x(block, step):
    return lax.ppermute(block, "narrow", [(i, (i + step) % NX) for i in range(NX)])


def after(block, *earlier):
    return lax.optimization_barrier((block, *earlier))[0]


def halves(block):
    high = lax.reduce_precision(block, 8, 7)
    return high.astype(jnp.bfloat16), (block - high).astype(jnp.bfloat16)


def on_device(stored_amps, integrals, pair_counts, block_map):
    place = lax.axis_index("wide")
    layer = lax.axis_index("narrow")
    core = place % NC
    my_y = (place // NC) % NY
    my_z = place // (NC * NY)
    width = stored_amps.shape[1]

    sibling = other_core(stored_amps)
    theirs = jnp.concatenate(
        [other_core(after(part, sibling)) for part in jnp.split(integrals, 4)], axis=0
    )
    top, low = stored_amps[:BR], stored_amps[BR:]

    def by_core(mine, others):
        return jnp.concatenate(
            [jnp.where(core == 0, mine, others), jnp.where(core == 0, others, mine)], axis=0
        )

    tops = by_core(top, sibling[:BR])
    lows = by_core(low, sibling[BR:])

    def mine_of(block):
        size = block.shape[0] // NC
        return lax.dynamic_slice_in_dim(block, core * size, size, 0)

    live = jnp.arange(width, dtype=jnp.int32)[:, None] < pair_counts[layer]
    held = jnp.where(live, jnp.concatenate([integrals, theirs], axis=1), jnp.float32(0.0))
    held_high, held_low = halves(held)

    def times(pieces):
        high, low_part = halves(jnp.concatenate(pieces, axis=0))
        count = high.shape[0]
        big = jnp.dot(
            jnp.concatenate([high, low_part], axis=0),
            held_high,
            preferred_element_type=jnp.float32,
        )
        small = jnp.dot(high, held_low, preferred_element_type=jnp.float32)
        return big[:count] + (big[count:] + small)

    t1 = along_z(tops)
    l1 = along_y(lows)
    t2 = along_z(t1)
    l2 = along_y(mine_of(l1))
    first = jnp.concatenate([top, t1], axis=0)
    f1 = along_y(after(first, l1))
    row_own = jnp.concatenate([low, l1, l2], axis=0)
    row_other = other_core(row_own)
    t3 = along_z(t2)
    a1 = along_z(after(row_own, t2))
    t4 = along_z(mine_of(t3))
    second = jnp.concatenate([t2, t3, t4], axis=0)
    b1 = along_z(after(row_other, t3))
    f2 = along_y(after(f1, t3))
    s1 = along_y(second)
    a2 = along_z(a1)
    f3 = along_y(f2)
    b2 = along_z(b1)
    s2 = along_y(s1)
    near = times([first, second, f1, s1, row_own, by_core(a1, b1)])
    a3 = along_z(a2)
    b3 = along_z(after(b2, near))
    s3 = along_y(after(s2, a2, b2))
    middle = times([f2, s2, by_core(a2, b2)])
    a4 = along_z(after(a3, middle))
    span = NX * G

    def layer_sum(cycle):
        chunks = jnp.stack(
            [
                jnp.concatenate(
                    [cycle[:, a * G : (a + 1) * G], cycle[:, span + a * G : span + (a + 1) * G]],
                    axis=1,
                )
                for a in range(NX)
            ]
        )

        def chunk(step):
            return lax.dynamic_index_in_dim(chunks, (layer + step) % NX, 0, keepdims=False)

        total = chunk(0)
        for step in (1, 3, 2):
            total = total + along_x(chunk(step), step)
        return total

    early = layer_sum(jnp.concatenate([near, middle], axis=0))
    late = layer_sum(times([f3, s3, by_core(a3, b3), a4]))
    total = jnp.concatenate([early, late], axis=0)
    count = total.shape[0]
    total = jnp.where(core == 0, total, jnp.roll(total, G, axis=1))

    blocks = by_core(total, other_core(total)).reshape(NC * (count // BR), BR, 2 * G)

    target = jnp.arange(NZ * NY * NC, dtype=jnp.int32)
    pairs = target.shape[0] // 2
    owner = block_map[2 * (target % pairs) + core]
    their_core = owner % NC
    dz = (my_z - owner // (NC * NY)) % NZ
    dy = (my_y - (owner // NC) % NY) % NY
    is_top = target < pairs
    unit_low = jnp.array([0, 1, 3, 5], jnp.int32)[dy] + their_core * jnp.array(
        [4, 1, 4, 1], jnp.int32
    )[dy]
    side = jnp.where(is_top, their_core, unit_low // 4)
    holder = jnp.where(dz % 4 == 0, side, dz // 4)
    steps_z = jnp.where(holder == 0, dz, (NZ - dz) % NZ)
    steps_y = jnp.where(holder == 0, dy, (NY - dy) % NY)
    top_base = jnp.array([0, 8, 28, 44], jnp.int32)[steps_y]
    top_unit = jnp.where(
        steps_z == 0, 0, jnp.where(steps_z == 4, 7, 2 * steps_z - 1 + their_core)
    )
    low_base = jnp.array([16, 20, 36, 52, 60], jnp.int32)[steps_z]
    low_unit = jnp.where(steps_z % 4 == 0, unit_low % 4, unit_low)
    at = jnp.where(is_top, top_base + top_unit, low_base + low_unit) + holder * (count // BR)
    sent = jnp.take(blocks, at, axis=0, mode="clip")
    got = lax.all_to_all(sent, "wide", split_axis=0, concat_axis=0, tiled=True)
    got = got.reshape(NZ * NY, NC, BR, 2 * G)
    return jnp.transpose(got, (1, 2, 0, 3)).reshape(NC * BR, NZ * NY * 2 * G)


def solution(mesh):
    placed = (P("wide", "narrow"), P("narrow", "wide"), P(), P())
    return jax.shard_map(
        on_device, mesh=mesh, in_specs=placed, out_specs=P("wide", "narrow"), check_vma=False
    )
```
